32 devices in a mesh: fsdp: 4 (over y, core), ctx: 2 (over x), tp: 4 (over z).
Axes of the slice: x: 2, y: 2, z: 4, core: 2. Of those that a mesh axis runs over, the one named last changes fastest.
Arguments:
- block_input: bfloat16 [4096, 768], P(('fsdp', 'ctx', 'tp')), may hold values from -6 to 6
- cotangent: bfloat16 [4096, 768], P(('fsdp', 'ctx', 'tp'))
- norm1_gain: bfloat16 [768], replicated, may hold values from 0.25 to 1.75
- norm1_bias: bfloat16 [768], replicated, may hold values from -1.796875 to 1.796875
- norm2_gain: bfloat16 [768], replicated, may hold values from 0.25 to 1.75
- norm2_bias: bfloat16 [768], replicated, may hold values from -1.796875 to 1.796875
- qkv_weight: bfloat16 [3, 768, 768], P(None, ('fsdp', 'ctx'), 'tp')
- qkv_bias: bfloat16 [3, 768], P(None, 'tp'), may hold values from -3 to 3
- out_weight: bfloat16 [768, 768], P('tp', ('fsdp', 'ctx')), may hold values from -0.875 to 0.875
- out_bias: bfloat16 [768], replicated, may hold values from -1.796875 to 1.796875
- up_weight: bfloat16 [768, 3072], P(('fsdp', 'ctx'), 'tp'), may hold values from -0.21875 to 0.21875
- up_bias: bfloat16 [3072], P('tp'), may hold values from -3 to 3
- down_weight: bfloat16 [3072, 768], P('tp', ('fsdp', 'ctx')), may hold values from -0.109375 to 0.109375
- down_bias: bfloat16 [768], replicated, may hold values from -1.796875 to 1.796875
- doc_ids: int32 [4096], P(('fsdp', 'ctx')), may hold values from 0 to 7, as said below
- doc_start: int32 [4096], P(('fsdp', 'ctx')), may hold values from 0 to 1023, as said below
Outputs:
- block_output: bfloat16 [4096, 768], P(('fsdp', 'ctx', 'tp'))
- grad_input: bfloat16 [4096, 768], P(('fsdp', 'ctx', 'tp'))
- grad_qkv_weight: float32 [3, 768, 768], P(None, ('fsdp', 'ctx'), 'tp')
- grad_qkv_bias: float32 [3, 768], P(None, 'tp')
- grad_out_weight: float32 [768, 768], P('tp', ('fsdp', 'ctx'))
- grad_out_bias: float32 [768], replicated
- grad_up_weight: float32 [768, 3072], P(('fsdp', 'ctx'), 'tp')
- grad_up_bias: float32 [3072], P('tp')
- grad_down_weight: float32 [3072, 768], P('tp', ('fsdp', 'ctx'))
- grad_down_bias: float32 [768], replicated
- grad_norm1_gain: float32 [768], replicated
- grad_norm1_bias: float32 [768], replicated
- grad_norm2_gain: float32 [768], replicated
- grad_norm2_bias: float32 [768], replicated
The draws below stay inside these ranges and needn't reach their ends.
Inputs may be any that keep to these rules, and one draw needn't show every extreme that they name: `doc_ids`: numbers the documents of each sequence of 1024 tokens from 0 at the sequence's first token; within a sequence it never falls and rises by one at the first token of each document; a sequence holds at most 8 documents. `doc_start`: the position within its sequence of the first token of the token's document: 0 at each sequence's first token, a token's own position where its document begins, equal for all tokens of one document.
All inputs are finite; a program needn't handle non-finite values.
Results may differ from the reference program's by a relative error of at most 0.009.
Values may be sent and summed in bfloat16 or wider, within the bound.
A program may use at most 128 MiB of HBM per device.

```python
import jax
import jax.numpy as jnp
from jax import lax

D = 768
FF = 3072
HEADS = 12
HD = 64
ROT = 16
LEN = 1024
TOKENS = 4096


def document_layout(key):
    base_key = jax.random.fold_in(key, 4242)
    seq_count = TOKENS // LEN
    count_key = jax.random.fold_in(base_key, 1)
    order_key = jax.random.fold_in(base_key, 2)
    doc_counts = jax.random.randint(count_key, (seq_count,), 1, 9)
    first_flag = (jnp.arange(seq_count, dtype=jnp.int32) == 0).astype(jnp.int32)
    doc_counts = jnp.where(first_flag == 1, 8, doc_counts)
    extra = doc_counts - 1 - first_flag
    order_keys = jax.random.split(order_key, seq_count)
    ranks = jax.vmap(lambda one_key: jax.random.permutation(one_key, LEN - 2))(order_keys)
    inner = ranks < extra[:, None]
    head_col = jnp.ones((seq_count, 1), dtype=bool)
    tail_col = (first_flag == 1)[:, None]
    begins = jnp.concatenate([head_col, inner, tail_col], axis=1)
    column = jnp.arange(LEN, dtype=jnp.int32)[None, :]
    numbers = jnp.cumsum(begins.astype(jnp.int32), axis=1) - 1
    starts = lax.cummax(jnp.where(begins, column, 0), axis=1)
    return (numbers.reshape(TOKENS).astype(jnp.int32), starts.reshape(TOKENS).astype(jnp.int32))


def draw_doc_ids(key, part):
    return document_layout(key)[0]


def draw_doc_start(key, part):
    return document_layout(key)[1]


def draw_cotangent(key, part):
    row_scale = 0.5 + jnp.arange(TOKENS, dtype=jnp.float32)[:, None] / TOKENS
    sample = jax.random.normal(key, (TOKENS, D), jnp.float32)
    return (sample * row_scale).astype(jnp.bfloat16)


def draw_qkv_weight(key, part):
    sample = jax.random.normal(key, (3, D, D), jnp.float32) * D ** (-0.5)
    return sample.astype(jnp.bfloat16)


def levels(own_key, dims, cuts, least, largest):
    factor_of, own = 1.0, jax.random.fold_in(own_key, 6)
    for position, shards_of in cuts:
        steps = jnp.exp(jax.random.uniform(jax.random.fold_in(own, position), (shards_of,), jnp.float32, least / len(cuts), largest / len(cuts)))
        factor_of = factor_of * jnp.repeat(steps, dims[position] // shards_of).reshape([-1 if axis == position else 1 for axis in range(len(dims))])
    return factor_of


def centred(key, dims, spread, reach, shards=(), kind=jnp.bfloat16):
    factor_of = levels(key, dims, shards, -0.22, 0.18) if shards else 1.0
    values = jax.random.normal(key, dims, jnp.float32) * spread * factor_of
    return jnp.minimum(jnp.maximum(values, -reach), reach).astype(kind)


def setup_inputs(seed: int = 0) -> dict:
    streams_of = jax.random.split(jax.random.key(seed), 17)
    return {
        "block_input": centred(streams_of[0], (TOKENS, D), 1.0, 6.0, ((0, 32),)),
        "cotangent": draw_cotangent(jax.random.fold_in(streams_of[16], 71), 0),
        "norm1_gain": jnp.clip(1.0 + 0.15 * jax.random.normal(streams_of[2], (D,), jnp.float32), 0.25, 1.75).astype(jnp.bfloat16),
        "norm1_bias": centred(streams_of[3], (D,), 0.3, 1.796875),
        "norm2_gain": jnp.clip(1.0 + 0.15 * jax.random.normal(streams_of[4], (D,), jnp.float32), 0.25, 1.75).astype(jnp.bfloat16),
        "norm2_bias": centred(streams_of[5], (D,), 0.3, 1.796875),
        "qkv_weight": draw_qkv_weight(jax.random.fold_in(streams_of[16], 71), 0),
        "qkv_bias": centred(streams_of[7], (3, D), 0.5, 3.0, ((1, 4),)),
        "out_weight": centred(streams_of[8], (D, D), (D // 16) ** -0.5, 0.875, ((0, 4), (1, 8))),
        "out_bias": centred(streams_of[9], (D,), 0.3, 1.796875),
        "up_weight": centred(streams_of[10], (D, FF), D ** -0.5, 0.21875, ((0, 8), (1, 4))),
        "up_bias": centred(streams_of[11], (FF,), 0.5, 3.0, ((0, 4),)),
        "down_weight": centred(streams_of[12], (FF, D), FF ** -0.5, 0.109375, ((0, 4), (1, 8))),
        "down_bias": centred(streams_of[13], (D,), 0.3, 1.796875),
        "doc_ids": draw_doc_ids(jax.random.fold_in(streams_of[16], 71), 0),
        "doc_start": draw_doc_start(jax.random.fold_in(streams_of[16], 71), 0),
    }


EPS = 1e-05

def gelu_parts(pre_act):
    cumulative = 0.5 * (1.0 + jax.scipy.special.erf(pre_act * 0.7071067811865476))
    density = jnp.exp(-0.5 * pre_act * pre_act) * 0.3989422804014327
    return (pre_act * cumulative, cumulative + pre_act * density)

def angle_tables(offsets):
    half_rot = ROT // 2
    frequency = 10000.0 ** (-(2.0 * jnp.arange(half_rot, dtype=jnp.float32)) / ROT)
    angles = offsets.astype(jnp.float32)[:, None] * frequency[None, :]
    angles = jnp.concatenate([angles, angles], axis=1)
    return (jnp.cos(angles), jnp.sin(angles))

def rotate(tensor, cosine, sine_table):
    half_rot = ROT // 2
    turned = jnp.concatenate([-tensor[..., half_rot:ROT], tensor[..., :half_rot]], axis=-1)
    leading = tensor[..., :ROT] * cosine[:, None, :] + turned * sine_table[:, None, :]
    return jnp.concatenate([leading, tensor[..., ROT:]], axis=-1)

def normalize(rows_in):
    centered = rows_in - lax.optimization_barrier(jnp.mean(rows_in, axis=1, keepdims=True))
    inv_std = lax.rsqrt(lax.optimization_barrier(jnp.mean(centered * centered, axis=1, keepdims=True)) + EPS)
    return (centered * inv_std, inv_std)

def attention_probs(queries, keys_all, query_pos, query_doc, key_doc):
    score_scale = HD ** (-0.5)
    scores = jnp.einsum('qhd,khd->hqk', queries, keys_all) * score_scale
    key_pos = jnp.arange(keys_all.shape[0], dtype=jnp.int32)
    allowed = (query_doc[:, None] == key_doc[None, :]) & (key_pos[None, :] <= query_pos[:, None])
    masked = jnp.where(allowed[None], scores, -1e+30)
    row_peak = lax.optimization_barrier(jnp.max(masked, axis=2, keepdims=True))
    exponent = jnp.where(allowed[None], jnp.exp(masked - row_peak), 0.0)
    return exponent / lax.optimization_barrier(jnp.sum(exponent, axis=2, keepdims=True))

def reference(block_input, cotangent, norm1_gain, norm1_bias, norm2_gain, norm2_bias, qkv_weight, qkv_bias, out_weight, out_bias, up_weight, up_bias, down_weight, down_bias, doc_ids, doc_start):
    seq_count = TOKENS // LEN
    score_scale = HD ** (-0.5)
    gain_one = norm1_gain.astype(jnp.float32)
    bias_one = norm1_bias.astype(jnp.float32)
    gain_two = norm2_gain.astype(jnp.float32)
    bias_two = norm2_bias.astype(jnp.float32)

    def one_sequence(totals, pieces):
        seq_in, seq_cot, seq_doc, seq_start = pieces
        seq_float = seq_in.astype(jnp.float32)
        normed, inv_std = normalize(seq_float)
        first_in = (normed * gain_one + bias_one).astype(jnp.bfloat16)
        second_in = (normed * gain_two + bias_two).astype(jnp.bfloat16)
        projected = jnp.stack([jnp.dot(first_in, qkv_weight[part_idx], preferred_element_type=jnp.float32) for part_idx in range(3)])
        projected = projected + qkv_bias.astype(jnp.float32)[:, None, :]
        positions = jnp.arange(LEN, dtype=jnp.int32)
        cosine, sine_table = angle_tables(positions - seq_start)
        queries = rotate(projected[0].reshape(LEN, HEADS, HD), cosine, sine_table).astype(jnp.bfloat16)
        keys_all = rotate(projected[1].reshape(LEN, HEADS, HD), cosine, sine_table).astype(jnp.bfloat16)
        values_all = projected[2].reshape(LEN, HEADS, HD).astype(jnp.bfloat16)
        attn_probs = attention_probs(queries.astype(jnp.float32), keys_all.astype(jnp.float32), positions, seq_doc, seq_doc)
        probs_b = attn_probs.astype(jnp.bfloat16)
        attended = jnp.einsum('hqk,khd->qhd', probs_b.astype(jnp.float32), values_all.astype(jnp.float32)).reshape(LEN, D).astype(jnp.bfloat16)
        pre_act = jnp.dot(second_in, up_weight, preferred_element_type=jnp.float32) + up_bias.astype(jnp.float32)
        activated, gelu_slope = gelu_parts(pre_act)
        act_b = activated.astype(jnp.bfloat16)
        branches = jnp.dot(attended, out_weight, preferred_element_type=jnp.float32) + jnp.dot(act_b, down_weight, preferred_element_type=jnp.float32)
        out_rows = (seq_float + branches + out_bias.astype(jnp.float32) + down_bias.astype(jnp.float32)).astype(jnp.bfloat16)
        cot_float = seq_cot.astype(jnp.float32)
        bias_grad = lax.optimization_barrier(jnp.sum(cot_float, axis=0))
        grad_out_w = jnp.dot(attended.T, seq_cot, preferred_element_type=jnp.float32)
        grad_down_w = jnp.dot(act_b.T, seq_cot, preferred_element_type=jnp.float32)
        d_attended = jnp.dot(seq_cot, out_weight.T, preferred_element_type=jnp.float32).astype(jnp.bfloat16)
        d_pre = (jnp.dot(seq_cot, down_weight.T, preferred_element_type=jnp.float32) * gelu_slope).astype(jnp.bfloat16)
        grad_up_w = jnp.dot(second_in.T, d_pre, preferred_element_type=jnp.float32)
        grad_up_b = lax.optimization_barrier(jnp.sum(d_pre.astype(jnp.float32), axis=0))
        d_second = jnp.dot(d_pre, up_weight.T, preferred_element_type=jnp.float32)
        d_heads = d_attended.astype(jnp.float32).reshape(LEN, HEADS, HD)
        d_values = jnp.einsum('hqk,qhd->khd', probs_b.astype(jnp.float32), d_heads)
        d_probs = jnp.einsum('qhd,khd->hqk', d_heads, values_all.astype(jnp.float32))
        delta_sum = lax.optimization_barrier(jnp.sum(attn_probs * d_probs, axis=2, keepdims=True))
        d_scores = (attn_probs * (d_probs - delta_sum)).astype(jnp.bfloat16)
        d_query = jnp.einsum('hqk,khd->qhd', d_scores.astype(jnp.float32), keys_all.astype(jnp.float32)) * score_scale
        d_keys = jnp.einsum('hqk,qhd->khd', d_scores.astype(jnp.float32), queries.astype(jnp.float32)) * score_scale
        d_qkv = jnp.stack([rotate(d_query, cosine, -sine_table).reshape(LEN, D), rotate(d_keys, cosine, -sine_table).reshape(LEN, D), d_values.reshape(LEN, D)]).astype(jnp.bfloat16)
        grad_qkv_b = lax.optimization_barrier(jnp.sum(d_qkv.astype(jnp.float32), axis=1))
        grad_qkv_w = jnp.stack([jnp.dot(first_in.T, d_qkv[part_idx], preferred_element_type=jnp.float32) for part_idx in range(3)])
        d_first = jnp.dot(d_qkv[0], qkv_weight[0].T, preferred_element_type=jnp.float32)
        d_first = d_first + jnp.dot(d_qkv[1], qkv_weight[1].T, preferred_element_type=jnp.float32)
        d_first = d_first + jnp.dot(d_qkv[2], qkv_weight[2].T, preferred_element_type=jnp.float32)
        combined = d_first * gain_one + d_second * gain_two
        mean_one = lax.optimization_barrier(jnp.mean(combined, axis=1, keepdims=True))
        mean_two = lax.optimization_barrier(jnp.mean(combined * normed, axis=1, keepdims=True))
        grad_rows = (cot_float + inv_std * (combined - mean_one - normed * mean_two)).astype(jnp.bfloat16)
        terms = (grad_qkv_w, grad_qkv_b, grad_out_w, bias_grad, grad_up_w, grad_up_b, grad_down_w, lax.optimization_barrier(jnp.sum(d_first * normed, axis=0)), lax.optimization_barrier(jnp.sum(d_first, axis=0)), lax.optimization_barrier(jnp.sum(d_second * normed, axis=0)), lax.optimization_barrier(jnp.sum(d_second, axis=0)))
        new_totals = tuple((total + term for total, term in zip(totals, terms)))
        return (new_totals, (out_rows, grad_rows))
    start_totals = (jnp.zeros((3, D, D), jnp.float32), jnp.zeros((3, D), jnp.float32), jnp.zeros((D, D), jnp.float32), jnp.zeros((D,), jnp.float32), jnp.zeros((D, FF), jnp.float32), jnp.zeros((FF,), jnp.float32), jnp.zeros((FF, D), jnp.float32), jnp.zeros((D,), jnp.float32), jnp.zeros((D,), jnp.float32), jnp.zeros((D,), jnp.float32), jnp.zeros((D,), jnp.float32))
    sequences = (block_input.reshape(seq_count, LEN, D), cotangent.reshape(seq_count, LEN, D), doc_ids.reshape(seq_count, LEN), doc_start.reshape(seq_count, LEN))
    totals, stacked = lax.scan(one_sequence, start_totals, sequences)
    block_output = stacked[0].reshape(TOKENS, D)
    grad_input = stacked[1].reshape(TOKENS, D)
    return (block_output, grad_input, totals[0], totals[1], totals[2], totals[3], totals[4], totals[5], totals[6], totals[3], totals[7], totals[8], totals[9], totals[10])
```

```python
import jax
import jax.numpy as jnp
from jax import lax
from jax.experimental import pallas as pl
from jax.experimental.pallas import tpu as pltpu
import functools
from jax.sharding import PartitionSpec as P

HD = 64
ROT = 16


EPS = 1e-05


def gelu_parts(pre_act):
    cumulative = 0.5 * (1.0 + jax.scipy.special.erf(pre_act * 0.7071067811865476))
    density = jnp.exp(-0.5 * pre_act * pre_act) * 0.3989422804014327
    return (pre_act * cumulative, cumulative + pre_act * density)


def angle_tables(offsets):
    half_rot = ROT // 2
    frequency = 10000.0 ** (-(2.0 * jnp.arange(half_rot, dtype=jnp.float32)) / ROT)
    angles = offsets.astype(jnp.float32)[:, None] * frequency[None, :]
    angles = jnp.concatenate([angles, angles], axis=1)
    return (jnp.cos(angles), jnp.sin(angles))


def rotate(tensor, cosine, sine_table):
    half_rot = ROT // 2
    turned = jnp.concatenate([-tensor[..., half_rot:ROT], tensor[..., :half_rot]], axis=-1)
    leading = tensor[..., :ROT] * cosine[:, None, :] + turned * sine_table[:, None, :]
    return jnp.concatenate([leading, tensor[..., ROT:]], axis=-1)


def normalize(rows_in):
    centered = rows_in - jnp.mean(rows_in, axis=1, keepdims=True)
    inv_std = lax.rsqrt(jnp.mean(centered * centered, axis=1, keepdims=True) + EPS)
    return (centered * inv_std, inv_std)


MESH = pl.DeviceIdType.MESH
VMEM = pl.BlockSpec(memory_space=pltpu.VMEM)
ANY = pl.BlockSpec(memory_space=pl.ANY)
PLANE = ("fsdp", "ctx")


def position():
    f = lax.axis_index("fsdp")
    return lax.rem(f, 2), f // 2, lax.axis_index("ctx"), lax.axis_index("tp")


def partner():
    core, y, _, _ = position()
    return {"fsdp": y * 2 + 1 - core}


def x_peer():
    return {"ctx": 1 - lax.axis_index("ctx")}


def y_peer():
    core, y, _, _ = position()
    return {"fsdp": (1 - y) * 2 + core}


def plane_peer(step):
    rank = lax.rem(lax.axis_index("fsdp") * 2 + lax.axis_index("ctx") + step, 8)
    return {"fsdp": rank // 2, "ctx": lax.rem(rank, 2)}


def z_peer(step, count):
    return {"tp": lax.rem(lax.axis_index("tp") + step, count)}


def greet(peers):
    barrier = pltpu.get_barrier_semaphore()
    for peer in peers:
        pl.semaphore_signal(barrier, inc=1, device_id=peer, device_id_type=MESH)
    pl.semaphore_wait(barrier, len(peers))


def remote(src, dst, sems, k, peer):
    return pltpu.make_async_remote_copy(
        src_ref=src,
        dst_ref=dst,
        send_sem=sems[0].at[k],
        recv_sem=sems[1].at[k],
        device_id=peer,
        device_id_type=MESH,
    )


def run_all(*parts):
    parts = list(parts)
    while parts:
        parts = [part for part in parts if next(part, "end") != "end"]


def plane_gather(src, out, sems, own_sem):
    core, y, x, _ = position()
    half = src.shape[0] // 2
    first, second = pl.ds(0, half), pl.ds(half, half)

    def slot(yy, xx):
        return (yy * 2 + core) * 2 + xx

    own, from_x, from_y, diag = slot(y, x), slot(y, 1 - x), slot(1 - y, x), slot(1 - y, 1 - x)
    to_p, to_x, to_y = partner(), x_peer(), y_peer()

    def piece(k, where, rows, peer):
        place = out.at[where, rows]
        return remote(src.at[rows] if k < 4 else place, place, sems, k, peer)

    sends = [
        piece(0, own, first, to_x),
        piece(1, own, second, to_y),
        piece(2, own, second, to_x),
        piece(3, own, first, to_y),
    ]
    whole = remote(src, out.at[own], sems, 4, to_p)
    keep = pltpu.make_async_copy(src, out.at[own], own_sem)
    for copy in sends:
        copy.start()
    whole.start()
    keep.start()
    yield
    relays = [
        (0, [(5, from_x, first, to_y), (7, from_x, first, to_p)]),
        (1, [(6, from_y, second, to_x), (8, from_y, second, to_p)]),
        (2, [(9, from_x, second, to_p)]),
        (3, [(10, from_y, first, to_p)]),
    ]
    later = []
    for k, nexts in relays:
        sends[k].wait_recv()
        for args in nexts:
            copy = piece(*args)
            copy.start()
            later.append(copy)
        if k == 1:
            yield
    by_key = {5: later[0], 6: later[2]}
    yield
    for k, args in ((5, (11, diag, first, to_p)), (6, (12, diag, second, to_p))):
        by_key[k].wait_recv()
        copy = piece(*args)
        copy.start()
        later.append(copy)
    yield
    for copy in later:
        if copy is not by_key[5] and copy is not by_key[6]:
            copy.wait_recv()
    whole.wait_recv()
    for copy in sends + later + [whole]:
        copy.wait_send()
    keep.wait()


def z_gather(src, out, ups, downs, own_sem, count):
    t = lax.axis_index("tp")
    keep = pltpu.make_async_copy(src, out.at[t], own_sem)

    def up(s):
        where = out.at[jnp.maximum(t - s, 0)]
        peer = {"tp": jnp.minimum(t + 1, count - 1)}
        return remote(src if s == 0 else where, where, ups, s, peer)

    def down(s):
        where = out.at[jnp.minimum(t + s, count - 1)]
        peer = {"tp": jnp.maximum(t - 1, 0)}
        return remote(src if s == 0 else where, where, downs, s, peer)

    for s in range(count):
        if s > 0:

            @pl.when(t - s >= 0)
            def _():
                up(s - 1).wait_recv()

            @pl.when(t + s <= count - 1)
            def _():
                down(s - 1).wait_recv()

        if s < count - 1:

            @pl.when((t - s >= 0) & (t < count - 1))
            def _():
                up(s).start()

            @pl.when((t + s <= count - 1) & (t > 0))
            def _():
                down(s).start()

            if s == 0:
                keep.start()
            yield
    for s in range(count - 1):

        @pl.when((t - s >= 0) & (t < count - 1))
        def _():
            up(s).wait_send()

        @pl.when((t + s <= count - 1) & (t > 0))
        def _():
            down(s).wait_send()

    keep.wait()


def x_gather(src, out, sems, own_sem):
    x = lax.axis_index("ctx")
    copy = remote(src, out.at[x], sems, 0, x_peer())
    keep = pltpu.make_async_copy(src, out.at[x], own_sem)
    copy.start()
    keep.start()
    yield
    yield
    yield
    copy.wait()
    keep.wait()


def x_swap(src, out, sems):
    copy = remote(src.at[1 - lax.axis_index("ctx")], out, sems, 0, x_peer())
    copy.start()
    yield
    yield
    copy.wait()


def plane_scatter(src, out, core_in, summed, side_in, mixed, last_in, sems):
    core, y, x, _ = position()
    half = out.shape[0] // 2
    rows = (pl.ds(0, half), pl.ds(half, half))
    to_p, to_x, to_y = partner(), x_peer(), y_peer()
    wide = jnp.float32
    first = []
    for q in range(4):
        there = ((q // 2) * 2 + 1 - core) * 2 + q % 2
        first.append(remote(src.at[there], core_in.at[q], sems, q, to_p))
    for copy in first:
        copy.start()
    yield
    for q in range(4):
        first[q].wait_recv()
        here = ((q // 2) * 2 + core) * 2 + q % 2
        summed[q] = (src[here].astype(wide) + core_in[q].astype(wide)).astype(summed.dtype)
    second = [
        remote(summed.at[(1 - y) * 2 + 1 - x, rows[0]], side_in.at[0], sems, 4, to_x),
        remote(summed.at[(1 - y) * 2 + 1 - x, rows[1]], side_in.at[1], sems, 5, to_y),
        remote(summed.at[y * 2 + 1 - x, rows[0]], side_in.at[2], sems, 6, to_x),
        remote(summed.at[(1 - y) * 2 + x, rows[1]], side_in.at[3], sems, 7, to_y),
    ]
    for copy in second:
        copy.start()
    yield
    third = []
    for k, (where, peer) in enumerate((((1 - y) * 2 + x, to_y), (y * 2 + 1 - x, to_x))):
        second[k].wait_recv()
        total = summed[where, rows[k]].astype(wide) + side_in[k].astype(wide)
        mixed[k] = total.astype(mixed.dtype)
        copy = remote(mixed.at[k], last_in.at[k], sems, 8 + k, peer)
        copy.start()
        third.append(copy)
    yield
    for k in range(2):
        second[2 + k].wait_recv()
        third[k].wait_recv()
        out[rows[k]] = (
            summed[y * 2 + x, rows[k]].astype(wide)
            + side_in[2 + k].astype(wide)
            + last_in[k].astype(wide)
        )
    for copy in first + second + third:
        copy.wait_send()


def z_scatter(src, out, landed, sems, count):
    t = lax.axis_index("tp")
    copies = []
    for d in range(1, count):
        peer = z_peer(d, count)
        copies.append(remote(src.at[peer["tp"]], landed.at[d - 1], sems, d - 1, peer))
    for copy in copies:
        copy.start()
    yield
    yield
    yield
    total = src[t].astype(jnp.float32)
    for d in range(1, count):
        copies[d - 1].wait()
        total = total + landed[d - 1].astype(jnp.float32)
    out[...] = total


def small_sum(src, out, z_in, middle, plane_in, z_sems, plane_sems, count, shared):
    t = lax.axis_index("tp")
    rank = lax.axis_index("fsdp") * 2 + lax.axis_index("ctx")
    ones = [remote(src, z_in.at[t], z_sems, d - 1, z_peer(d, count)) for d in range(1, count)]
    for copy in ones:
        copy.start()
    z_in[t] = src[...]
    yield
    for copy in ones:
        copy.wait()
    total = z_in[0]
    for i in range(1, count):
        total = total + z_in[i]
    row = lax.broadcasted_iota(jnp.int32, total.shape, 0)
    middle[...] = jnp.where(row < shared, total, src[...])
    twos = [remote(middle, plane_in.at[rank], plane_sems, d - 1, plane_peer(d)) for d in range(1, 8)]
    for copy in twos:
        copy.start()
    plane_in[rank] = middle[...]
    yield
    yield
    for copy in twos:
        copy.wait()
    total = plane_in[0]
    for i in range(1, 8):
        total = total + plane_in[i]
    out[...] = total


def near_peers(count):
    return [partner(), x_peer(), y_peer()] + [z_peer(d, count) for d in range(1, count)]


def sem_pair(count):
    return [pltpu.SemaphoreType.DMA((count,)), pltpu.SemaphoreType.DMA((count,))]


def call(body, outs, out_specs, inputs, scratch, collective):
    return pl.pallas_call(
        body,
        out_shape=outs,
        in_specs=[VMEM] * len(inputs),
        out_specs=out_specs,
        scratch_shapes=scratch,
        compiler_params=pltpu.CompilerParams(
            collective_id=collective, has_side_effects=True, vmem_limit_bytes=48 * 1024 * 1024
        ),
    )(*inputs)


def shape(dims, dtype=jnp.bfloat16):
    return jax.ShapeDtypeStruct(dims, dtype)


def gather_first(weights, rows, count):
    def body(w, r, wf, rf, a, b, c, d, e, g, own):
        greet(near_peers(count))
        run_all(
            z_gather(r, rf, (c, d), (e, g), own.at[0], count),
            plane_gather(w, wf, (a, b), own.at[1]),
        )

    return call(
        body,
        [shape((8,) + weights.shape), shape((count,) + rows.shape)],
        [ANY, ANY],
        (weights, rows),
        sem_pair(13) + sem_pair(count) + sem_pair(count) + [pltpu.SemaphoreType.DMA((2,))],
        0,
    )


def gather_second(rows, keys, count):
    def body(r, k, rf, kf, a, b, c, d, e, g, own):
        greet(near_peers(count))
        run_all(
            z_gather(r, rf, (c, d), (e, g), own.at[0], count),
            x_gather(k, kf, (a, b), own.at[1]),
        )

    return call(
        body,
        [shape((count,) + rows.shape), shape((2,) + keys.shape)],
        [ANY, ANY],
        (rows, keys),
        sem_pair(1) + sem_pair(count) + sem_pair(count) + [pltpu.SemaphoreType.DMA((2,))],
        1,
    )


def scatter_scratch(block):
    rows, lanes = block
    half = rows // 2
    return [
        pltpu.VMEM((4, rows, lanes), jnp.bfloat16),
        pltpu.VMEM((4, rows, lanes), jnp.bfloat16),
        pltpu.VMEM((4, half, lanes), jnp.bfloat16),
        pltpu.VMEM((2, half, lanes), jnp.bfloat16),
        pltpu.VMEM((2, half, lanes), jnp.bfloat16),
    ] + sem_pair(10)


def scatter_first(grads, partial, key_grads, count):
    def body(g, p, k, go, po, ko, a, b, c, d, e, s0, s1, land, z0, z1, x0, x1):
        greet(near_peers(count))
        run_all(
            plane_scatter(g, go, a, b, c, d, e, (s0, s1)),
            x_swap(k, ko, (x0, x1)),
            z_scatter(p, po, land, (z0, z1), count),
        )

    return call(
        body,
        [
            shape(grads.shape[1:], jnp.float32),
            shape(partial.shape[1:], jnp.float32),
            shape(key_grads.shape[1:]),
        ],
        [VMEM] * 3,
        (grads, partial, key_grads),
        scatter_scratch(grads.shape[1:])
        + [pltpu.VMEM((count - 1,) + partial.shape[1:], jnp.bfloat16)]
        + sem_pair(count)
        + sem_pair(1),
        2,
    )


def scatter_second(grads, partial, small, count, shared):
    def body(g, p, m, go, po, mo, a, b, c, d, e, s0, s1, land, z0, z1, zi, mid, pi, m0, m1, n0, n1):
        greet(
            [plane_peer(i) for i in range(1, 8)] + [z_peer(i, count) for i in range(1, count)]
        )
        run_all(
            small_sum(m, mo, zi, mid, pi, (m0, m1), (n0, n1), count, shared),
            plane_scatter(g, go, a, b, c, d, e, (s0, s1)),
            z_scatter(p, po, land, (z0, z1), count),
        )

    return call(
        body,
        [
            shape(grads.shape[1:], jnp.float32),
            shape(partial.shape[1:], jnp.float32),
            shape(small.shape, jnp.float32),
        ],
        [VMEM] * 3,
        (grads, partial, small),
        scatter_scratch(grads.shape[1:])
        + [pltpu.VMEM((count - 1,) + partial.shape[1:], jnp.bfloat16)]
        + sem_pair(count)
        + [
            pltpu.VMEM((count,) + small.shape, jnp.float32),
            pltpu.VMEM(small.shape, jnp.float32),
            pltpu.VMEM((8,) + small.shape, jnp.float32),
        ]
        + sem_pair(count)
        + sem_pair(7),
        3,
    )


def plain_gather_first(weights, rows, count):
    return lax.all_gather(weights, PLANE), lax.all_gather(rows, "tp")


def plain_gather_second(rows, keys, count):
    return lax.all_gather(rows, "tp"), lax.all_gather(keys, "ctx")


def plain_scatter(grads, partial):
    grads = lax.psum_scatter(grads.astype(jnp.float32), PLANE, scatter_dimension=0)
    return grads, lax.psum_scatter(partial.astype(jnp.float32), "tp", scatter_dimension=0)


def plain_scatter_first(grads, partial, key_grads, count):
    x = lax.axis_index("ctx")
    total = lax.psum_scatter(key_grads.astype(jnp.float32), "ctx", scatter_dimension=0)
    own = lax.dynamic_index_in_dim(key_grads, x, 0, keepdims=False)
    return plain_scatter(grads, partial) + (total - own.astype(jnp.float32),)


def plain_scatter_second(grads, partial, small, count, shared):
    total = lax.psum(small, PLANE)
    return plain_scatter(grads, partial) + (
        jnp.concatenate([lax.psum(total[:shared], "tp"), total[shared:]]),
    )


def attention_probs(queries, keys_all, query_pos, query_start):
    score_scale = HD ** (-0.5)
    scores = (
        jnp.einsum("qhd,khd->hqk", queries, keys_all, preferred_element_type=jnp.float32)
        * score_scale
    )
    key_pos = jnp.arange(keys_all.shape[0], dtype=jnp.int32)
    allowed = (key_pos[None, :] >= query_start[:, None]) & (key_pos[None, :] <= query_pos[:, None])
    masked = jnp.where(allowed[None], scores, -1e30)
    row_peak = jnp.max(masked, axis=2, keepdims=True)
    exponent = jnp.where(allowed[None], jnp.exp(masked - row_peak), 0.0)
    return exponent / jnp.sum(exponent, axis=2, keepdims=True)


def dot(a, b, dims=((1,), (0,))):
    return lax.dot_general(a, b, (dims, ((), ())), preferred_element_type=jnp.float32)


def local(
    sizes,
    block_input,
    cotangent,
    norm1_gain,
    norm1_bias,
    norm2_gain,
    norm2_bias,
    qkv_weight,
    qkv_bias,
    out_weight,
    out_bias,
    up_weight,
    up_bias,
    down_weight,
    down_bias,
    doc_ids,
    doc_start,
):
    fsdp, ctx, count = sizes
    if fsdp == 4 and ctx == 2 and count > 1:
        comm = (gather_first, gather_second, scatter_first, scatter_second)
    else:
        comm = (plain_gather_first, plain_gather_second, plain_scatter_first, plain_scatter_second)
    wide, narrow = jnp.float32, jnp.bfloat16
    own_count, width = block_input.shape
    lw = qkv_weight.shape[2]
    hidden = up_weight.shape[1]
    heads_here = lw // HD
    row_count = own_count * count
    group = fsdp * ctx
    score_scale = HD ** (-0.5)
    piece = qkv_weight.shape[1]
    packed = jnp.concatenate(
        [qkv_weight[0], qkv_weight[1], qkv_weight[2], out_weight.T, up_weight, down_weight.T],
        axis=1,
    )
    packed, full_in = comm[0](packed, block_input, count)
    packed = packed.reshape(width, packed.shape[2])
    full_in = full_in.reshape(row_count, width)
    qkv_full = packed[:, : 3 * lw]
    out_t = packed[:, 3 * lw : 4 * lw]
    up_full = packed[:, 4 * lw : 4 * lw + hidden]
    down_t = packed[:, 4 * lw + hidden :]
    gain_one = norm1_gain.astype(wide)
    gain_two = norm2_gain.astype(wide)
    normed, inv_std = normalize(full_in.astype(wide))
    first_in = (normed * gain_one + norm1_bias.astype(wide)).astype(narrow)
    second_in = (normed * gain_two + norm2_bias.astype(wide)).astype(narrow)
    projected = dot(first_in, qkv_full) + qkv_bias.astype(wide).reshape(1, 3 * lw)
    query_pos = lax.axis_index("ctx") * row_count + jnp.arange(row_count, dtype=jnp.int32)
    cosine, sine_table = angle_tables(query_pos - doc_start)
    queries = rotate(
        projected[:, :lw].reshape(row_count, heads_here, HD), cosine, sine_table
    ).astype(narrow)
    keys_here = rotate(
        projected[:, lw : 2 * lw].reshape(row_count, heads_here, HD), cosine, sine_table
    ).astype(narrow)
    keys_values = jnp.concatenate(
        [keys_here.reshape(row_count, lw), projected[:, 2 * lw :].astype(narrow)], axis=1
    )
    full_cot, keys_values = comm[1](cotangent, keys_values, count)
    full_cot = full_cot.reshape(row_count, width)
    length = ctx * row_count
    keys_values = keys_values.reshape(length, 2 * lw)
    keys_all = keys_values[:, :lw].reshape(length, heads_here, HD)
    values_all = keys_values[:, lw:].reshape(length, heads_here, HD)
    attn_probs = attention_probs(queries, keys_all, query_pos, doc_start)
    probs_b = attn_probs.astype(narrow)
    attended = jnp.einsum("hqk,khd->qhd", probs_b, values_all, preferred_element_type=wide)
    attended = attended.reshape(row_count, lw).astype(narrow)
    pre_act = dot(second_in, up_full) + up_bias.astype(wide)
    activated, gelu_slope = gelu_parts(pre_act)
    act_b = activated.astype(narrow)
    last = ((1,), (1,))
    rows = ((0,), (0,))
    forward = dot(attended, out_t, last) + dot(act_b, down_t, last)
    d_attended = dot(full_cot, out_t).astype(narrow)
    d_pre = (dot(full_cot, down_t) * gelu_slope).astype(narrow)
    grad_up_local = dot(second_in, d_pre, rows)
    grad_down_local = dot(full_cot, act_b, rows)
    up_bias_grad = jnp.sum(d_pre.astype(wide), axis=0)
    d_heads = d_attended.reshape(row_count, heads_here, HD)
    d_values = jnp.einsum("hqk,qhd->khd", probs_b, d_heads, preferred_element_type=wide)
    d_probs = jnp.einsum("qhd,khd->hqk", d_heads, values_all, preferred_element_type=wide)
    delta_sum = jnp.sum(attn_probs * d_probs, axis=2, keepdims=True)
    d_scores = (attn_probs * (d_probs - delta_sum)).astype(narrow)
    d_query = (
        jnp.einsum("hqk,khd->qhd", d_scores, keys_all, preferred_element_type=wide) * score_scale
    )
    d_keys = (
        jnp.einsum("hqk,qhd->khd", d_scores, queries, preferred_element_type=wide) * score_scale
    )
    key_grads = jnp.concatenate([d_keys.reshape(length, lw), d_values.reshape(length, lw)], axis=1)
    key_grads = key_grads.reshape(ctx, row_count, 2 * lw)
    mlp_grads, summed, key_far = comm[2](
        jnp.concatenate([grad_up_local.astype(narrow), grad_down_local.astype(narrow)], axis=1)
        .reshape(group, piece, 2 * hidden),
        forward.astype(narrow).reshape(count, own_count, width),
        key_grads.astype(narrow),
        count,
    )
    block_output = (
        block_input.astype(wide) + summed + out_bias.astype(wide) + down_bias.astype(wide)
    ).astype(narrow)
    key_own = lax.dynamic_index_in_dim(key_grads, lax.axis_index("ctx"), 0, keepdims=False)
    key_own = key_own + key_far.astype(wide)
    d_qkv = jnp.concatenate(
        [
            rotate(d_query, cosine, -sine_table).reshape(row_count, lw),
            rotate(
                key_own[:, :lw].reshape(row_count, heads_here, HD), cosine, -sine_table
            ).reshape(row_count, lw),
            key_own[:, lw:],
        ],
        axis=1,
    ).astype(narrow)
    qkv_bias_grad = jnp.sum(d_qkv.astype(wide), axis=0)
    grad_qkv_local = dot(first_in, d_qkv, rows)
    grad_out_local = dot(full_cot, attended, rows)
    d_first = dot(d_qkv, qkv_full, last)
    d_second = dot(d_pre, up_full, last)
    cot_float = cotangent.astype(wide)
    span = max(width, hidden, 3 * lw)

    def pad(row):
        return jnp.pad(row, (0, span - row.shape[0]))

    small = jnp.stack(
        [
            pad(row)
            for row in (
                jnp.sum(cot_float, axis=0),
                jnp.sum(d_first * normed, axis=0),
                jnp.sum(d_first, axis=0),
                jnp.sum(d_second * normed, axis=0),
                jnp.sum(d_second, axis=0),
                up_bias_grad,
                qkv_bias_grad,
                jnp.zeros((width,), wide),
            )
        ]
    )
    partial = d_first * gain_one + d_second * gain_two
    attn_grads, combined, small = comm[3](
        jnp.concatenate([grad_qkv_local.astype(narrow), grad_out_local.astype(narrow)], axis=1)
        .reshape(group, piece, 4 * lw),
        partial.astype(narrow).reshape(count, own_count, width),
        small,
        count,
        5,
    )
    normed_own, inv_own = normalize(block_input.astype(wide))
    mean_one = jnp.mean(combined, axis=1, keepdims=True)
    mean_two = jnp.mean(combined * normed_own, axis=1, keepdims=True)
    grad_input = (cot_float + inv_own * (combined - mean_one - normed_own * mean_two)).astype(narrow)
    return (
        block_output,
        grad_input,
        attn_grads[:, : 3 * lw].reshape(piece, 3, lw).transpose(1, 0, 2),
        small[6, : 3 * lw].reshape(3, lw),
        attn_grads[:, 3 * lw :].T,
        small[0, :width],
        mlp_grads[:, :hidden],
        small[5, :hidden],
        mlp_grads[:, hidden:].T,
        small[0, :width],
        small[1, :width],
        small[2, :width],
        small[3, :width],
        small[4, :width],
    )


def solution(mesh):
    in_specs = (
        P(("fsdp", "ctx", "tp"), None),
        P(("fsdp", "ctx", "tp"), None),
        P(),
        P(),
        P(),
        P(),
        P(None, ("fsdp", "ctx"), "tp"),
        P(None, "tp"),
        P("tp", ("fsdp", "ctx")),
        P(),
        P(("fsdp", "ctx"), "tp"),
        P("tp"),
        P("tp", ("fsdp", "ctx")),
        P(),
        P(("fsdp", "ctx")),
        P(("fsdp", "ctx")),
    )
    out_specs = (
        P(("fsdp", "ctx", "tp"), None),
        P(("fsdp", "ctx", "tp"), None),
        P(None, ("fsdp", "ctx"), "tp"),
        P(None, "tp"),
        P("tp", ("fsdp", "ctx")),
        P(),
        P(("fsdp", "ctx"), "tp"),
        P("tp"),
        P("tp", ("fsdp", "ctx")),
        P(),
        P(),
        P(),
        P(),
        P(),
    )
    sizes = tuple(mesh.shape[axis] for axis in ("fsdp", "ctx", "tp"))
    body = functools.partial(local, sizes)
    return jax.shard_map(body, mesh=mesh, in_specs=in_specs, out_specs=out_specs, check_vma=False)
```

```python
import jax
import jax.numpy as jnp
from jax import lax
from jax.experimental import pallas as pl
from jax.experimental.pallas import tpu as pltpu
import functools
from jax.sharding import PartitionSpec as P

HD = 64
ROT = 16


EPS = 1e-05


def gelu_parts(pre_act):
    cumulative = 0.5 * (1.0 + jax.scipy.special.erf(pre_act * 0.7071067811865476))
    density = jnp.exp(-0.5 * pre_act * pre_act) * 0.3989422804014327
    return (pre_act * cumulative, cumulative + pre_act * density)


def angle_tables(offsets):
    half_rot = ROT // 2
    frequency = 10000.0 ** (-(2.0 * jnp.arange(half_rot, dtype=jnp.float32)) / ROT)
    angles = offsets.astype(jnp.float32)[:, None] * frequency[None, :]
    angles = jnp.concatenate([angles, angles], axis=1)
    return (jnp.cos(angles), jnp.sin(angles))


def rotate(tensor, cosine, sine_table):
    half_rot = ROT // 2
    turned = jnp.concatenate([-tensor[..., half_rot:ROT], tensor[..., :half_rot]], axis=-1)
    leading = tensor[..., :ROT] * cosine[:, None, :] + turned * sine_table[:, None, :]
    return jnp.concatenate([leading, tensor[..., ROT:]], axis=-1)


def normalize(rows_in):
    centered = rows_in - jnp.mean(rows_in, axis=1, keepdims=True)
    inv_std = lax.rsqrt(jnp.mean(centered * centered, axis=1, keepdims=True) + EPS)
    return (centered * inv_std, inv_std)


MESH = pl.DeviceIdType.MESH
VMEM = pl.BlockSpec(memory_space=pltpu.VMEM)
ANY = pl.BlockSpec(memory_space=pl.ANY)
PLANE = ("fsdp", "ctx")


def position():
    f = lax.axis_index("fsdp")
    return lax.rem(f, 2), f // 2, lax.axis_index("ctx"), lax.axis_index("tp")


def partner():
    core, y, _, _ = position()
    return {"fsdp": y * 2 + 1 - core}


def x_peer():
    return {"ctx": 1 - lax.axis_index("ctx")}


def y_peer():
    core, y, _, _ = position()
    return {"fsdp": (1 - y) * 2 + core}


def plane_peer(step):
    rank = lax.rem(lax.axis_index("fsdp") * 2 + lax.axis_index("ctx") + step, 8)
    return {"fsdp": rank // 2, "ctx": lax.rem(rank, 2)}


def z_peer(step, count):
    return {"tp": lax.rem(lax.axis_index("tp") + step, count)}


def greet(peers):
    barrier = pltpu.get_barrier_semaphore()
    for peer in peers:
        pl.semaphore_signal(barrier, inc=1, device_id=peer, device_id_type=MESH)
    pl.semaphore_wait(barrier, len(peers))


def remote(src, dst, sems, k, peer):
    return pltpu.make_async_remote_copy(
        src_ref=src,
        dst_ref=dst,
        send_sem=sems[0].at[k],
        recv_sem=sems[1].at[k],
        device_id=peer,
        device_id_type=MESH,
    )


def run_all(*parts):
    parts = list(parts)
    while parts:
        parts = [part for part in parts if next(part, "end") != "end"]


def plane_gather(src, out, sems, own_sem):
    core, y, x, _ = position()
    half = src.shape[0] // 2
    first, second = pl.ds(0, half), pl.ds(half, half)

    def slot(yy, xx):
        return (yy * 2 + core) * 2 + xx

    own, from_x, from_y, diag = slot(y, x), slot(y, 1 - x), slot(1 - y, x), slot(1 - y, 1 - x)
    to_p, to_x, to_y = partner(), x_peer(), y_peer()

    def piece(k, where, rows, peer):
        place = out.at[where, rows]
        return remote(src.at[rows] if k < 4 else place, place, sems, k, peer)

    sends = [
        piece(0, own, first, to_x),
        piece(1, own, second, to_y),
        piece(2, own, second, to_x),
        piece(3, own, first, to_y),
    ]
    whole = remote(src, out.at[own], sems, 4, to_p)
    keep = pltpu.make_async_copy(src, out.at[own], own_sem)
    for copy in sends:
        copy.start()
    whole.start()
    keep.start()
    yield
    relays = [
        (0, [(5, from_x, first, to_y), (7, from_x, first, to_p)]),
        (1, [(6, from_y, second, to_x), (8, from_y, second, to_p)]),
        (2, [(9, from_x, second, to_p)]),
        (3, [(10, from_y, first, to_p)]),
    ]
    later = []
    for k, nexts in relays:
        sends[k].wait_recv()
        for args in nexts:
            copy = piece(*args)
            copy.start()
            later.append(copy)
        if k == 1:
            yield
    by_key = {5: later[0], 6: later[2]}
    yield
    for k, args in ((5, (11, diag, first, to_p)), (6, (12, diag, second, to_p))):
        by_key[k].wait_recv()
        copy = piece(*args)
        copy.start()
        later.append(copy)
    yield
    for copy in later:
        if copy is not by_key[5] and copy is not by_key[6]:
            copy.wait_recv()
    whole.wait_recv()
    for copy in sends + later + [whole]:
        copy.wait_send()
    keep.wait()


def z_gather(src, out, ups, downs, own_sem, count):
    t = lax.axis_index("tp")
    keep = pltpu.make_async_copy(src, out.at[t], own_sem)

    def up(s):
        where = out.at[jnp.maximum(t - s, 0)]
        peer = {"tp": jnp.minimum(t + 1, count - 1)}
        return remote(src if s == 0 else where, where, ups, s, peer)

    def down(s):
        where = out.at[jnp.minimum(t + s, count - 1)]
        peer = {"tp": jnp.maximum(t - 1, 0)}
        return remote(src if s == 0 else where, where, downs, s, peer)

    for s in range(count):
        if s == count - 1:
            yield
        if s > 0:

            @pl.when(t - s >= 0)
            def _():
                up(s - 1).wait_recv()

            @pl.when(t + s <= count - 1)
            def _():
                down(s - 1).wait_recv()

        if s < count - 1:

            @pl.when((t - s >= 0) & (t < count - 1))
            def _():
                up(s).start()

            @pl.when((t + s <= count - 1) & (t > 0))
            def _():
                down(s).start()

            if s == 0:
                keep.start()
            yield
    for s in range(count - 1):

        @pl.when((t - s >= 0) & (t < count - 1))
        def _():
            up(s).wait_send()

        @pl.when((t + s <= count - 1) & (t > 0))
        def _():
            down(s).wait_send()

    keep.wait()


def head_lanes(h, base=0):
    return slice(base + h * HD, base + (h + 1) * HD)


def row_tiles(rows):
    return 2 if rows % 32 == 0 else 1


def attend(queries, keys, values, starts, out, first_row, wait):
    wait()
    rows, lw = queries.shape
    tile = rows // row_tiles(rows)
    for h in range(lw // HD):
        for r in range(0, rows, tile):
            here = pl.ds(r, tile)
            probs = head_probs(
                queries[here, head_lanes(h)], keys(h), starts[here, :], first_row + r
            )
            out[here, head_lanes(h)] = dot(probs.astype(jnp.bfloat16), values(h)).astype(
                jnp.bfloat16
            )
    yield


def x_gather_attend(src, out, sems, own_sem, queries, starts, attended):
    x = lax.axis_index("ctx")
    rows, lanes = src.shape
    copy = remote(src, out.at[x], sems, 0, x_peer())
    keep = pltpu.make_async_copy(src, out.at[x], own_sem)
    copy.start()
    keep.start()
    yield
    yield
    yield
    yield

    def wait():
        copy.wait()
        keep.wait()

    def keys(h):
        return out[:, :, head_lanes(h)].reshape(2 * rows, HD)

    def values(h):
        return out[:, :, head_lanes(h, lanes // 2)].reshape(2 * rows, HD)

    yield from attend(queries, keys, values, starts, attended, x * rows, wait)


def attend_back(queries, kv, d_out, starts, d_query, key_sum, total, far, landed, sems):
    x = lax.axis_index("ctx")
    rows, lw = queries.shape
    tile = rows // row_tiles(rows)
    yield
    for h in range(lw // HD):
        keys = kv[:, head_lanes(h)]
        values = kv[:, head_lanes(h, lw)]
        for r in range(0, rows, tile):
            here = pl.ds(r, tile)
            dq, dk, dv = head_back(
                queries[here, head_lanes(h)],
                keys,
                values,
                d_out[here, head_lanes(h)],
                starts[here, :],
                x * rows + r,
            )
            d_query[here, head_lanes(h)] = dq
            if r == 0:
                total[:, head_lanes(h)] = dk
                total[:, head_lanes(h, lw)] = dv
            else:
                total[:, head_lanes(h)] += dk
                total[:, head_lanes(h, lw)] += dv
            yield
    away = pl.ds(pl.multiple_of((1 - x) * rows, rows), rows)
    near = pl.ds(pl.multiple_of(x * rows, rows), rows)
    far[...] = total[away, :].astype(far.dtype)
    copy = remote(far, landed, sems, 0, x_peer())
    copy.start()
    yield
    copy.wait()
    key_sum[...] = total[near, :] + landed[...].astype(jnp.float32)


def plane_scatter(src, out, core_in, summed, side_in, mixed, last_in, sems):
    core, y, x, _ = position()
    half = out.shape[0] // 2
    rows = (pl.ds(0, half), pl.ds(half, half))
    to_p, to_x, to_y = partner(), x_peer(), y_peer()
    wide = jnp.float32
    first = []
    for q in range(4):
        there = ((q // 2) * 2 + 1 - core) * 2 + q % 2
        first.append(remote(src.at[there], core_in.at[q], sems, q, to_p))
    for copy in first:
        copy.start()
    yield
    for q in range(4):
        first[q].wait_recv()
        here = ((q // 2) * 2 + core) * 2 + q % 2
        summed[q] = (src[here].astype(wide) + core_in[q].astype(wide)).astype(summed.dtype)
    second = [
        remote(summed.at[(1 - y) * 2 + 1 - x, rows[0]], side_in.at[0], sems, 4, to_x),
        remote(summed.at[(1 - y) * 2 + 1 - x, rows[1]], side_in.at[1], sems, 5, to_y),
        remote(summed.at[y * 2 + 1 - x, rows[0]], side_in.at[2], sems, 6, to_x),
        remote(summed.at[(1 - y) * 2 + x, rows[1]], side_in.at[3], sems, 7, to_y),
    ]
    for copy in second:
        copy.start()
    yield
    third = []
    for k, (where, peer) in enumerate((((1 - y) * 2 + x, to_y), (y * 2 + 1 - x, to_x))):
        second[k].wait_recv()
        total = summed[where, rows[k]].astype(wide) + side_in[k].astype(wide)
        mixed[k] = total.astype(mixed.dtype)
        copy = remote(mixed.at[k], last_in.at[k], sems, 8 + k, peer)
        copy.start()
        third.append(copy)
    yield
    for k in range(2):
        second[2 + k].wait_recv()
        third[k].wait_recv()
        out[rows[k]] = (
            summed[y * 2 + x, rows[k]].astype(wide)
            + side_in[2 + k].astype(wide)
            + last_in[k].astype(wide)
        )
    for copy in first + second + third:
        copy.wait_send()


def z_scatter(src, out, up_in, down_in, up_mix, down_mix, ups, downs, count):
    t = lax.axis_index("tp")
    above = {"tp": jnp.minimum(t + 1, count - 1)}
    below = {"tp": jnp.maximum(t - 1, 0)}
    wide = jnp.float32

    def up(b, from_ref):
        return remote(from_ref.at[b], up_in.at[b], ups, b, above)

    def down(b, from_ref):
        return remote(from_ref.at[b], down_in.at[b], downs, b, below)

    @pl.when(t == 0)
    def _():
        for b in range(count - 1, 0, -1):
            up(b, src).start()

    @pl.when(t == count - 1)
    def _():
        for b in range(count - 1):
            down(b, src).start()

    yield
    for i in range(count - 2):
        b = count - 1 - i

        @pl.when((t < b) & (t > 0))
        def _():
            up(b, up_mix).wait_recv()
            up_mix[b] = (src[b].astype(wide) + up_in[b].astype(wide)).astype(up_mix.dtype)
            up(b, up_mix).start()

        @pl.when((t > i) & (t < count - 1))
        def _():
            down(i, down_mix).wait_recv()
            down_mix[i] = (src[i].astype(wide) + down_in[i].astype(wide)).astype(down_mix.dtype)
            down(i, down_mix).start()

        yield
    out[...] = src[t].astype(wide)
    for b in range(count):
        if b > 0:

            @pl.when(t == b)
            def _():
                up(b, up_mix).wait_recv()
                out[...] += up_in[b].astype(wide)

            @pl.when(t < b)
            def _():
                up(b, up_mix).wait_send()

        if b < count - 1:

            @pl.when(t == b)
            def _():
                down(b, down_mix).wait_recv()
                out[...] += down_in[b].astype(wide)

            @pl.when(t > b)
            def _():
                down(b, down_mix).wait_send()


def z_scratch(block, count):
    return [pltpu.VMEM((count,) + block, jnp.bfloat16)] * 4 + sem_pair(count) + sem_pair(count)


def small_sum(src, out, z_in, middle, plane_in, z_sems, plane_sems, count, shared):
    t = lax.axis_index("tp")
    rank = lax.axis_index("fsdp") * 2 + lax.axis_index("ctx")
    ones = [remote(src, z_in.at[t], z_sems, d - 1, z_peer(d, count)) for d in range(1, count)]
    for copy in ones:
        copy.start()
    z_in[t] = src[...]
    yield
    for copy in ones:
        copy.wait()
    total = z_in[0]
    for i in range(1, count):
        total = total + z_in[i]
    row = lax.broadcasted_iota(jnp.int32, total.shape, 0)
    middle[...] = jnp.where(row < shared, total, src[...])
    twos = [remote(middle, plane_in.at[rank], plane_sems, d - 1, plane_peer(d)) for d in range(1, 8)]
    for copy in twos:
        copy.start()
    plane_in[rank] = middle[...]
    yield
    yield
    for copy in twos:
        copy.wait()
    total = plane_in[0]
    for i in range(1, 8):
        total = total + plane_in[i]
    out[...] = total


def near_peers(count):
    return [partner(), x_peer(), y_peer()] + [z_peer(d, count) for d in range(1, count)]


def sem_pair(count):
    return [pltpu.SemaphoreType.DMA((count,)), pltpu.SemaphoreType.DMA((count,))]


def call(body, outs, out_specs, inputs, scratch, collective):
    return pl.pallas_call(
        body,
        out_shape=outs,
        in_specs=[VMEM] * len(inputs),
        out_specs=out_specs,
        scratch_shapes=scratch,
        compiler_params=pltpu.CompilerParams(
            collective_id=collective, has_side_effects=True, vmem_limit_bytes=48 * 1024 * 1024
        ),
    )(*inputs)


def shape(dims, dtype=jnp.bfloat16):
    return jax.ShapeDtypeStruct(dims, dtype)


def gather_first(weights, rows, count):
    def body(w, r, wf, rf, a, b, c, d, e, g, own):
        greet(near_peers(count))
        run_all(
            z_gather(r, rf, (c, d), (e, g), own.at[0], count),
            plane_gather(w, wf, (a, b), own.at[1]),
        )

    return call(
        body,
        [shape((8,) + weights.shape), shape((count,) + rows.shape)],
        [ANY, ANY],
        (weights, rows),
        sem_pair(13) + sem_pair(count) + sem_pair(count) + [pltpu.SemaphoreType.DMA((2,))],
        0,
    )


def gather_second(weights, rows, keys, queries, starts, count):
    def body(w, r, k, q, st, wf, rf, kf, at, w0, w1, a, b, c, d, e, g, own):
        greet(near_peers(count))
        run_all(
            x_gather_attend(k, kf, (a, b), own.at[1], q, st, at),
            plane_gather(w, wf, (w0, w1), own.at[2]),
            z_gather(r, rf, (c, d), (e, g), own.at[0], count),
        )

    return call(
        body,
        [
            shape((8,) + weights.shape),
            shape((count,) + rows.shape),
            shape((2,) + keys.shape),
            shape(queries.shape),
        ],
        [ANY, ANY, VMEM, VMEM],
        (weights, rows, keys, queries, starts),
        sem_pair(13)
        + sem_pair(1)
        + sem_pair(count)
        + sem_pair(count)
        + [pltpu.SemaphoreType.DMA((3,))],
        1,
    )


def scatter_scratch(block):
    rows, lanes = block
    half = rows // 2
    return [
        pltpu.VMEM((4, rows, lanes), jnp.bfloat16),
        pltpu.VMEM((4, rows, lanes), jnp.bfloat16),
        pltpu.VMEM((4, half, lanes), jnp.bfloat16),
        pltpu.VMEM((2, half, lanes), jnp.bfloat16),
        pltpu.VMEM((2, half, lanes), jnp.bfloat16),
    ] + sem_pair(10)


def scatter_first(grads, partial, queries, kv, d_out, starts, count):
    def body(
        g, p, q, k, do, st, go, po, dq, ks,
        a, b, c, d, e, s0, s1, z0, z1, z2, z3, u0, u1, v0, v1, total, far, land, x0, x1,
    ):
        greet(near_peers(count))
        run_all(
            z_scatter(p, po, z0, z1, z2, z3, (u0, u1), (v0, v1), count),
            plane_scatter(g, go, a, b, c, d, e, (s0, s1)),
            attend_back(q, k, do, st, dq, ks, total, far, land, (x0, x1)),
        )

    rows, lw = queries.shape
    return call(
        body,
        [
            shape(grads.shape[1:], jnp.float32),
            shape(partial.shape[1:], jnp.float32),
            shape(queries.shape, jnp.float32),
            shape((rows, 2 * lw), jnp.float32),
        ],
        [VMEM] * 4,
        (grads, partial, queries, kv, d_out, starts),
        scatter_scratch(grads.shape[1:])
        + z_scratch(partial.shape[1:], count)
        + [
            pltpu.VMEM(kv.shape, jnp.float32),
            pltpu.VMEM((rows, 2 * lw), jnp.bfloat16),
            pltpu.VMEM((rows, 2 * lw), jnp.bfloat16),
        ]
        + sem_pair(1),
        2,
    )


def scatter_second(grads, partial, small, count, shared):
    def body(
        g, p, m, go, po, mo,
        a, b, c, d, e, s0, s1, z0, z1, z2, z3, u0, u1, v0, v1, zi, mid, pi, m0, m1, n0, n1,
    ):
        greet(
            [plane_peer(i) for i in range(1, 8)] + [z_peer(i, count) for i in range(1, count)]
        )
        run_all(
            small_sum(m, mo, zi, mid, pi, (m0, m1), (n0, n1), count, shared),
            plane_scatter(g, go, a, b, c, d, e, (s0, s1)),
            z_scatter(p, po, z0, z1, z2, z3, (u0, u1), (v0, v1), count),
        )

    return call(
        body,
        [
            shape(grads.shape[1:], jnp.float32),
            shape(partial.shape[1:], jnp.float32),
            shape(small.shape, jnp.float32),
        ],
        [VMEM] * 3,
        (grads, partial, small),
        scatter_scratch(grads.shape[1:])
        + z_scratch(partial.shape[1:], count)
        + [
            pltpu.VMEM((count,) + small.shape, jnp.float32),
            pltpu.VMEM(small.shape, jnp.float32),
            pltpu.VMEM((8,) + small.shape, jnp.float32),
        ]
        + sem_pair(count)
        + sem_pair(7),
        3,
    )


def plain_gather_first(weights, rows, count):
    return lax.all_gather(weights, PLANE), lax.all_gather(rows, "tp")


def plain_gather_second(weights, rows, keys, queries, starts, count):
    kv = lax.all_gather(keys, "ctx")
    whole = kv.reshape(-1, keys.shape[1])
    lw = queries.shape[1]
    first_row = lax.axis_index("ctx") * queries.shape[0]
    heads = []
    for h in range(lw // HD):
        probs = head_probs(queries[:, head_lanes(h)], whole[:, head_lanes(h)], starts, first_row)
        heads.append(dot(probs.astype(jnp.bfloat16), whole[:, head_lanes(h, lw)]))
    attended = jnp.concatenate(heads, axis=1).astype(jnp.bfloat16)
    return lax.all_gather(weights, PLANE), lax.all_gather(rows, "tp"), kv, attended


def plain_scatter(grads, partial):
    grads = lax.psum_scatter(grads.astype(jnp.float32), PLANE, scatter_dimension=0)
    return grads, lax.psum_scatter(partial.astype(jnp.float32), "tp", scatter_dimension=0)


def plain_scatter_first(grads, partial, queries, kv, d_out, starts, count):
    rows, lw = queries.shape
    first_row = lax.axis_index("ctx") * rows
    heads = [
        head_back(
            queries[:, head_lanes(h)],
            kv[:, head_lanes(h)],
            kv[:, head_lanes(h, lw)],
            d_out[:, head_lanes(h)],
            starts,
            first_row,
        )
        for h in range(lw // HD)
    ]
    d_query = jnp.concatenate([head[0] for head in heads], axis=1)
    total = jnp.concatenate([head[1] for head in heads] + [head[2] for head in heads], axis=1)
    total = lax.psum_scatter(total, "ctx", scatter_dimension=0, tiled=True)
    return plain_scatter(grads, partial) + (d_query, total)


def plain_scatter_second(grads, partial, small, count, shared):
    total = lax.psum(small, PLANE)
    return plain_scatter(grads, partial) + (
        jnp.concatenate([lax.psum(total[:shared], "tp"), total[shared:]]),
    )


def head_probs(queries, keys, starts, first_row):
    scores = dot(queries, keys, ((1,), (1,))) * HD ** (-0.5)
    query_pos = first_row + lax.broadcasted_iota(jnp.int32, scores.shape, 0)
    key_pos = lax.broadcasted_iota(jnp.int32, scores.shape, 1)
    masked = jnp.where((key_pos >= starts) & (key_pos <= query_pos), scores, -1e30)
    exponent = jnp.exp(masked - jnp.max(masked, axis=1, keepdims=True))
    return exponent * (1.0 / jnp.sum(exponent, axis=1, keepdims=True))


def head_back(queries, keys, values, d_out, starts, first_row):
    probs = head_probs(queries, keys, starts, first_row)
    d_probs = dot(d_out, values, ((1,), (1,)))
    delta = jnp.sum(probs * d_probs, axis=1, keepdims=True)
    d_scores = (probs * (d_probs - delta)).astype(jnp.bfloat16)
    scale = HD ** (-0.5)
    d_values = dot(probs.astype(jnp.bfloat16), d_out, ((0,), (0,)))
    return (
        dot(d_scores, keys) * scale,
        dot(d_scores, queries, ((0,), (0,))) * scale,
        d_values,
    )


def dot(a, b, dims=((1,), (0,))):
    return lax.dot_general(a, b, (dims, ((), ())), preferred_element_type=jnp.float32)


def local(
    sizes,
    block_input,
    cotangent,
    norm1_gain,
    norm1_bias,
    norm2_gain,
    norm2_bias,
    qkv_weight,
    qkv_bias,
    out_weight,
    out_bias,
    up_weight,
    up_bias,
    down_weight,
    down_bias,
    doc_ids,
    doc_start,
):
    fsdp, ctx, count = sizes
    if fsdp == 4 and ctx == 2 and count > 1:
        comm = (gather_first, gather_second, scatter_first, scatter_second)
    else:
        comm = (plain_gather_first, plain_gather_second, plain_scatter_first, plain_scatter_second)
    wide, narrow = jnp.float32, jnp.bfloat16
    own_count, width = block_input.shape
    lw = qkv_weight.shape[2]
    hidden = up_weight.shape[1]
    heads_here = lw // HD
    row_count = own_count * count
    group = fsdp * ctx
    piece = qkv_weight.shape[1]
    packed = jnp.concatenate(
        [qkv_weight[0], qkv_weight[1], qkv_weight[2], out_weight.T, up_weight], axis=1
    )
    packed, full_in = comm[0](packed, block_input, count)
    packed = packed.reshape(width, packed.shape[2])
    full_in = full_in.reshape(row_count, width)
    qkv_full = packed[:, : 3 * lw]
    out_t = packed[:, 3 * lw : 4 * lw]
    up_full = packed[:, 4 * lw :]
    gain_one = norm1_gain.astype(wide)
    gain_two = norm2_gain.astype(wide)
    normed, inv_std = normalize(full_in.astype(wide))
    first_in = (normed * gain_one + norm1_bias.astype(wide)).astype(narrow)
    second_in = (normed * gain_two + norm2_bias.astype(wide)).astype(narrow)
    projected = dot(first_in, qkv_full) + qkv_bias.astype(wide).reshape(1, 3 * lw)
    query_pos = lax.axis_index("ctx") * row_count + jnp.arange(row_count, dtype=jnp.int32)
    cosine, sine_table = angle_tables(query_pos - doc_start)
    queries = rotate(
        projected[:, :lw].reshape(row_count, heads_here, HD), cosine, sine_table
    ).astype(narrow)
    keys_here = rotate(
        projected[:, lw : 2 * lw].reshape(row_count, heads_here, HD), cosine, sine_table
    ).astype(narrow)
    keys_values = jnp.concatenate(
        [keys_here.reshape(row_count, lw), projected[:, 2 * lw :].astype(narrow)], axis=1
    )
    queries = queries.reshape(row_count, lw)
    starts = doc_start.reshape(row_count, 1)
    down_t, full_cot, keys_values, attended = comm[1](
        down_weight.T, cotangent, keys_values, queries, starts, count
    )
    down_t = down_t.reshape(width, hidden)
    full_cot = full_cot.reshape(row_count, width)
    keys_values = keys_values.reshape(ctx * row_count, 2 * lw)
    pre_act = dot(second_in, up_full) + up_bias.astype(wide)
    activated, gelu_slope = gelu_parts(pre_act)
    act_b = activated.astype(narrow)
    last = ((1,), (1,))
    rows = ((0,), (0,))
    forward = dot(attended, out_t, last) + dot(act_b, down_t, last)
    d_attended = dot(full_cot, out_t).astype(narrow)
    d_pre = (dot(full_cot, down_t) * gelu_slope).astype(narrow)
    grad_up_local = dot(second_in, d_pre, rows)
    grad_down_local = dot(full_cot, act_b, rows)
    up_bias_grad = jnp.sum(d_pre.astype(wide), axis=0)
    mlp_grads, summed, d_query, key_own = comm[2](
        jnp.concatenate([grad_up_local.astype(narrow), grad_down_local.astype(narrow)], axis=1)
        .reshape(group, piece, 2 * hidden),
        forward.astype(narrow).reshape(count, own_count, width),
        queries,
        keys_values,
        d_attended,
        starts,
        count,
    )
    block_output = (
        block_input.astype(wide) + summed + out_bias.astype(wide) + down_bias.astype(wide)
    ).astype(narrow)
    d_qkv = jnp.concatenate(
        [
            rotate(
                d_query.reshape(row_count, heads_here, HD), cosine, -sine_table
            ).reshape(row_count, lw),
            rotate(
                key_own[:, :lw].reshape(row_count, heads_here, HD), cosine, -sine_table
            ).reshape(row_count, lw),
            key_own[:, lw:],
        ],
        axis=1,
    ).astype(narrow)
    qkv_bias_grad = jnp.sum(d_qkv.astype(wide), axis=0)
    grad_qkv_local = dot(first_in, d_qkv, rows)
    grad_out_local = dot(full_cot, attended, rows)
    d_first = dot(d_qkv, qkv_full, last)
    d_second = dot(d_pre, up_full, last)
    cot_float = cotangent.astype(wide)
    span = max(width, hidden, 3 * lw)

    def pad(row):
        return jnp.pad(row, (0, span - row.shape[0]))

    small = jnp.stack(
        [
            pad(row)
            for row in (
                jnp.sum(cot_float, axis=0),
                jnp.sum(d_first * normed, axis=0),
                jnp.sum(d_first, axis=0),
                jnp.sum(d_second * normed, axis=0),
                jnp.sum(d_second, axis=0),
                up_bias_grad,
                qkv_bias_grad,
                jnp.zeros((width,), wide),
            )
        ]
    )
    partial = d_first * gain_one + d_second * gain_two
    attn_grads, combined, small = comm[3](
        jnp.concatenate([grad_qkv_local.astype(narrow), grad_out_local.astype(narrow)], axis=1)
        .reshape(group, piece, 4 * lw),
        partial.astype(narrow).reshape(count, own_count, width),
        small,
        count,
        5,
    )
    normed_own, inv_own = normalize(block_input.astype(wide))
    mean_one = jnp.mean(combined, axis=1, keepdims=True)
    mean_two = jnp.mean(combined * normed_own, axis=1, keepdims=True)
    grad_input = (cot_float + inv_own * (combined - mean_one - normed_own * mean_two)).astype(narrow)
    return (
        block_output,
        grad_input,
        attn_grads[:, : 3 * lw].reshape(piece, 3, lw).transpose(1, 0, 2),
        small[6, : 3 * lw].reshape(3, lw),
        attn_grads[:, 3 * lw :].T,
        small[0, :width],
        mlp_grads[:, :hidden],
        small[5, :hidden],
        mlp_grads[:, hidden:].T,
        small[0, :width],
        small[1, :width],
        small[2, :width],
        small[3, :width],
        small[4, :width],
    )


def solution(mesh):
    in_specs = (
        P(("fsdp", "ctx", "tp"), None),
        P(("fsdp", "ctx", "tp"), None),
        P(),
        P(),
        P(),
        P(),
        P(None, ("fsdp", "ctx"), "tp"),
        P(None, "tp"),
        P("tp", ("fsdp", "ctx")),
        P(),
        P(("fsdp", "ctx"), "tp"),
        P("tp"),
        P("tp", ("fsdp", "ctx")),
        P(),
        P(("fsdp", "ctx")),
        P(("fsdp", "ctx")),
    )
    out_specs = (
        P(("fsdp", "ctx", "tp"), None),
        P(("fsdp", "ctx", "tp"), None),
        P(None, ("fsdp", "ctx"), "tp"),
        P(None, "tp"),
        P("tp", ("fsdp", "ctx")),
        P(),
        P(("fsdp", "ctx"), "tp"),
        P("tp"),
        P("tp", ("fsdp", "ctx")),
        P(),
        P(),
        P(),
        P(),
        P(),
    )
    sizes = tuple(mesh.shape[axis] for axis in ("fsdp", "ctx", "tp"))
    body = functools.partial(local, sizes)
    return jax.shard_map(body, mesh=mesh, in_specs=in_specs, out_specs=out_specs, check_vma=False)
```
